32 devices in a mesh: row: 8 (over z, core), col: 4 (over y, x).
Axes of the slice: x: 2, y: 2, z: 4, core: 2. Of those that a mesh axis runs over, the one named last changes fastest.
Arguments:
- starting_state: float32 [4096, 256], P(('row', 'col')), may hold values from -1 to 1
- features: float32 [4096, 128], P(('row', 'col')), may hold values from -6 to 6
- cotangent: float32 [4096, 256], P(('row', 'col')), may hold values from -6 to 6
- degrees: int32 [4096], P(('row', 'col')), may hold values from 8 to 64
- tile_values: bfloat16 [8, 4, 4, 128, 128], P('row', 'col'), may hold values from 0 to 1, as said below
- tile_rows: int32 [8, 4, 4], P('row', 'col'), may hold values from 0 to 3, as said below
- tile_cols: int32 [8, 4, 4], P('row', 'col'), may hold values from 0 to 7, as said below
- tile_live: int32 [8, 4, 4], P('row', 'col'), may hold values from 0 to 1, as said below
- weight: float32 [256, 256], replicated, may hold values from -0.375 to 0.375
- input_map: float32 [128, 256], replicated, may hold values from -0.5 to 0.5
Outputs:
- states: float32 [4096, 256], P(('row', 'col'))
- adjoint: float32 [4096, 256], P(('row', 'col'))
- weight_grad: float32 [256, 256], replicated
- input_grad: float32 [128, 256], replicated
The draws below stay inside these ranges and needn't reach their ends.
Inputs may be any that keep to these rules, and one draw needn't show every extreme that they name: `tile_rows`: together with tile_cols, the slots of one device name distinct tiles. `tile_cols`: together with tile_rows, the slots of one device name distinct tiles. `tile_live`: on each device the live slots come first; every device has at least a quarter of its 4 slots live (and at least one), and some device has all 4 live. `tile_values`: roughly half of the entries of each tile are nonzero; nonzero weights lie in (0, 1].
All inputs are finite; a program needn't handle non-finite values.
Results may differ from the reference program's by a relative error of at most 0.012.
Values may be sent and summed in bfloat16 or wider, within the bound.
A program may use at most 64 MiB of HBM per device.

```python
import math
import jax
import jax.numpy as jnp
from jax import lax

WIDTH = 256
INPUTS = 128
BLOCK = 128
NODE_DEV = 128
ITERS = 1
NODES = 4096
TILE_ROWS = 4
TILE_COLS = 8
SLOTS = 4
N_ROW = 8
N_COL = 4


def tile_places(key):
    base = jax.random.fold_in(key, 101)
    keys = jax.random.split(base, N_ROW * N_COL)

    def one_device(device_key):
        return jax.random.permutation(device_key, TILE_ROWS * TILE_COLS)[:SLOTS]
    places = jax.vmap(one_device)(keys)
    return places.reshape(N_ROW, N_COL, SLOTS).astype(jnp.int32)


def draw_tile_rows(key, part):
    return (tile_places(key) // TILE_COLS).astype(jnp.int32)


def draw_tile_cols(key, part):
    return (tile_places(key) % TILE_COLS).astype(jnp.int32)


def draw_tile_live(key, part):
    base = jax.random.fold_in(key, 202)
    lowest = max(1, SLOTS // 4)
    first = jax.random.randint(base, (N_ROW * N_COL,), lowest, SLOTS + 1)
    second = jax.random.randint(jax.random.fold_in(base, 7), (N_ROW * N_COL,), lowest, SLOTS + 1)
    counts = jnp.minimum(first, second)
    chosen = jax.random.randint(jax.random.fold_in(base, 1), (), 0, N_ROW * N_COL)
    counts = jnp.where(jnp.arange(N_ROW * N_COL) == chosen, SLOTS, counts)
    live = (jnp.arange(SLOTS)[None, :] < counts[:, None]).astype(jnp.int32)
    return live.reshape(N_ROW, N_COL, SLOTS)


def draw_tile_values(key, part):
    base = jax.random.fold_in(key, 303)
    random_key_length, key_keep = jax.random.split(base, 2)
    shape = (N_ROW, N_COL, SLOTS, BLOCK, BLOCK)
    sizes_drawn = jnp.exp(jax.random.uniform(random_key_length, shape, jnp.float32, jnp.log(0.1), 0.0))
    keeping = jax.random.uniform(key_keep, shape, jnp.float32) < 0.5
    return jnp.where(keeping, sizes_drawn, 0.0).astype(jnp.bfloat16)


def with_ends(array, key, smallest, largest):
    shape = array.shape
    spot = [jax.random.randint(jax.random.fold_in(key, axis), (), 0, shape[axis]) for axis in range(len(shape))]
    array = array.at[tuple(spot)].set(smallest)
    longest = shape.index(max(shape))
    spot[longest] = (spot[longest] + 1) % shape[longest]
    return array.at[tuple(spot)].set(largest)


def shard_levels(stream_key, extent, shards, least, largest):
    def one(dim, shards_of):
        steps = jax.random.uniform(jax.random.fold_in(jax.random.fold_in(stream_key, 6), dim), (shards_of,), jnp.float32, least / len(shards), largest / len(shards))
        return jnp.repeat(jnp.exp(steps), extent[dim] // shards_of).reshape((-1,) + (1,) * (len(extent) - dim - 1))

    factor_of = one(*shards[0])
    for cut in shards[1:]:
        factor_of = factor_of * one(*cut)
    return factor_of


def scatter_about(rng, extent, scale, most, cuts=(), kind=jnp.bfloat16):
    gain = shard_levels(rng, extent, cuts, -0.22, 0.18) if cuts else 1.0
    entries = jax.random.normal(rng, extent, jnp.float32) * scale * gain
    return jnp.minimum(jnp.maximum(entries, -most), most).astype(kind)


def setup_inputs(seed: int = 0) -> dict:
    streams_of = jax.random.split(jax.random.key(seed), 11)
    return {
        "starting_state": jnp.clip(jax.random.uniform(streams_of[0], (NODES, WIDTH), jnp.float32, -1.0, 1.0) * shard_levels(streams_of[0], (NODES, WIDTH), ((0, 32),), -0.4, 0.0), -1.0, 1.0),
        "features": scatter_about(streams_of[1], (NODES, INPUTS), 1.0, 6.0, ((0, 32),), jnp.float32),
        "cotangent": scatter_about(streams_of[2], (NODES, WIDTH), 1.0, 6.0, ((0, 32),), jnp.float32),
        "degrees": with_ends(jax.random.randint(streams_of[3], (NODES,), 8, 65), jax.random.fold_in(streams_of[3], 1), 8, 64).astype(jnp.int32),
        "tile_values": draw_tile_values(jax.random.fold_in(streams_of[10], 71), 0),
        "tile_rows": draw_tile_rows(jax.random.fold_in(streams_of[10], 71), 0),
        "tile_cols": draw_tile_cols(jax.random.fold_in(streams_of[10], 71), 0),
        "tile_live": draw_tile_live(jax.random.fold_in(streams_of[10], 71), 0),
        "weight": scatter_about(streams_of[8], (WIDTH, WIDTH), WIDTH ** -0.5, 0.375, (), jnp.float32),
        "input_map": scatter_about(streams_of[9], (INPUTS, WIDTH), INPUTS ** -0.5, 0.5, (), jnp.float32),
    }


PRECISION_HIGH = lax.Precision.HIGHEST

def forward_partial(values, rows_here, cols_here, live_here, row_block):
    blocks = row_block.reshape(TILE_ROWS, BLOCK, WIDTH)
    picked = jnp.take(blocks, rows_here, axis=0).astype(jnp.float32)
    matrix_products = jnp.einsum('tab,taf->tbf', values.astype(jnp.float32), picked, precision=PRECISION_HIGH)
    columns = jnp.arange(TILE_COLS).astype(jnp.int32)
    tile_assignment = ((cols_here[:, None] == columns[None, :]) & (live_here[:, None] == 1)).astype(jnp.float32)
    partial_result_value = jnp.einsum('sl,sxm->lxm', tile_assignment, matrix_products, precision=PRECISION_HIGH)
    return partial_result_value.reshape(TILE_COLS * BLOCK, WIDTH).astype(jnp.bfloat16)

def adjoint_partial(values, rows_here, cols_here, live_here, col_block):
    blocks = col_block.reshape(TILE_COLS, BLOCK, WIDTH)
    picked = jnp.take(blocks, cols_here, axis=0).astype(jnp.float32)
    matrix_products = jnp.einsum('tab,tbf->taf', values.astype(jnp.float32), picked, precision=PRECISION_HIGH)
    sources = jnp.arange(TILE_ROWS).astype(jnp.int32)
    tile_assignment = ((rows_here[:, None] == sources[None, :]) & (live_here[:, None] == 1)).astype(jnp.float32)
    partial_result_value = jnp.einsum('tr,taf->raf', tile_assignment, matrix_products, precision=PRECISION_HIGH)
    return partial_result_value.reshape(TILE_ROWS * BLOCK, WIDTH).astype(jnp.bfloat16)

def forward_sum(scaled, tile_values, tile_rows, tile_cols, tile_live):
    layout = scaled.reshape(N_ROW, N_COL * NODE_DEV, WIDTH)

    def add_row(totals, row_index):

        def one_col(col_index):
            return forward_partial(tile_values[row_index, col_index], tile_rows[row_index, col_index], tile_cols[row_index, col_index], tile_live[row_index, col_index], layout[row_index])
        partials = lax.map(one_col, jnp.arange(N_COL).astype(jnp.int32))
        return (totals + partials.astype(jnp.float32), None)
    initial = jnp.zeros((N_COL, N_ROW * NODE_DEV, WIDTH), jnp.float32)
    totals, ignored = lax.scan(add_row, initial, jnp.arange(N_ROW).astype(jnp.int32))
    totals = totals.reshape(N_COL, N_ROW, NODE_DEV, WIDTH).transpose(1, 0, 2, 3)
    return totals.reshape(N_ROW * N_COL * NODE_DEV, WIDTH)

def adjoint_sum(scaled, tile_values, tile_rows, tile_cols, tile_live):
    layout = scaled.reshape(N_ROW, N_COL, NODE_DEV, WIDTH)

    def add_col(totals, col_index):
        col_block = lax.dynamic_index_in_dim(layout, col_index, 1, keepdims=False)
        col_block = col_block.reshape(N_ROW * NODE_DEV, WIDTH)

        def one_row(row_index):
            return adjoint_partial(tile_values[row_index, col_index], tile_rows[row_index, col_index], tile_cols[row_index, col_index], tile_live[row_index, col_index], col_block)
        partials = lax.map(one_row, jnp.arange(N_ROW).astype(jnp.int32))
        return (totals + partials.astype(jnp.float32), None)
    initial = jnp.zeros((N_ROW, N_COL * NODE_DEV, WIDTH), jnp.float32)
    totals, ignored = lax.scan(add_col, initial, jnp.arange(N_COL).astype(jnp.int32))
    return totals.reshape(N_ROW * N_COL * NODE_DEV, WIDTH)

def reference(starting_state, features, cotangent, degrees, tile_values, tile_rows, tile_cols, tile_live, weight, input_map):
    reciprocal_square_root = lax.rsqrt(degrees.astype(jnp.float32))[:, None]
    driving = jnp.dot(features, input_map, precision=PRECISION_HIGH)
    states = starting_state
    summed = starting_state
    for sweep in range(ITERS):
        scaled = (reciprocal_square_root * states).astype(jnp.bfloat16)
        summed = reciprocal_square_root * forward_sum(scaled, tile_values, tile_rows, tile_cols, tile_live)
        states = jnp.tanh(jnp.dot(summed, weight, precision=PRECISION_HIGH) + driving)
    slopes = 1.0 - states * states
    adjoint = cotangent
    for sweep in range(ITERS):
        scaled = (reciprocal_square_root * (slopes * adjoint)).astype(jnp.bfloat16)
        pulled = reciprocal_square_root * adjoint_sum(scaled, tile_values, tile_rows, tile_cols, tile_live)
        adjoint = cotangent + jnp.dot(pulled, weight.T, precision=PRECISION_HIGH)
    masked = slopes * adjoint
    factor = 1.0 / math.sqrt(NODES)
    weight_grad = jnp.dot(summed.T, masked, precision=PRECISION_HIGH) * factor
    input_grad = jnp.dot(features.T, masked, precision=PRECISION_HIGH) * factor
    return (states, adjoint, weight_grad, input_grad)
```

```python
import functools
import math

import jax
import jax.numpy as jnp
from jax import lax
from jax.experimental import pallas as pl
from jax.experimental.pallas import tpu as pltpu
from jax.sharding import PartitionSpec as P

PRECISION_HIGH = lax.Precision.HIGHEST
MESH = pl.DeviceIdType.MESH
VMEM_PLAN = 40 * 2**20
F32 = jnp.float32
BF16 = jnp.bfloat16


def spread(values, picked_at, label_at, live_here, gathered, out_count, equation):
    blocks = gathered.reshape(-1, values.shape[1], gathered.shape[1])
    picked = jnp.take(blocks, picked_at, axis=0)
    products = jnp.einsum(equation, values, picked, preferred_element_type=F32)
    labels = jnp.where(live_here == 1, label_at, out_count)
    return jax.ops.segment_sum(products, labels, num_segments=out_count)


def collective_path(
    starting_state, features, cotangent, degrees, tile_values,
    tile_rows, tile_cols, tile_live, weight, input_map,
):
    values, rows_here = tile_values[0, 0], tile_rows[0, 0]
    cols_here, live_here = tile_cols[0, 0], tile_live[0, 0]
    nodes, width = starting_state.shape
    block = values.shape[1]
    n_row, n_col = lax.axis_size("row"), lax.axis_size("col")
    inverse_root = lax.rsqrt(degrees.astype(F32))[:, None]
    driving = jnp.dot(features, input_map, precision=PRECISION_HIGH)
    scaled = (inverse_root * starting_state).astype(BF16)
    gathered = lax.all_gather(scaled, "col", axis=0, tiled=True)
    partial = spread(
        values, rows_here, cols_here, live_here, gathered, n_row * nodes // block, "tab,taf->tbf"
    )
    partial = partial.reshape(n_row * nodes, width).astype(BF16)
    own = lax.psum_scatter(partial, "row", scatter_dimension=0, tiled=True).astype(F32)
    summed = inverse_root * own
    states = jnp.tanh(jnp.dot(summed, weight, precision=PRECISION_HIGH) + driving)
    slopes = 1.0 - states * states
    scaled = (inverse_root * (slopes * cotangent)).astype(BF16)
    gathered = lax.all_gather(scaled, "row", axis=0, tiled=True)
    partial = spread(
        values, cols_here, rows_here, live_here, gathered, n_col * nodes // block, "tab,tbf->taf"
    )
    partial = partial.reshape(n_col * nodes, width).astype(BF16)
    own = lax.psum_scatter(partial, "col", scatter_dimension=0, tiled=True).astype(F32)
    pulled = inverse_root * own
    adjoint = cotangent + jnp.dot(pulled, weight.T, precision=PRECISION_HIGH)
    masked = slopes * adjoint
    factor = 1.0 / math.sqrt(nodes * n_row * n_col)
    weight_part = jnp.dot(summed.T, masked, precision=PRECISION_HIGH)
    input_part = jnp.dot(features.T, masked, precision=PRECISION_HIGH)
    weight_grad, input_grad = lax.psum((weight_part, input_part), ("row", "col"))
    return states, adjoint, weight_grad * factor, input_grad * factor


def kernel(
    n_row, n_col, factor,
    state_ref, feat_ref, cot_ref, deg_ref, val_ref, rows_ref, cols_ref, live_ref, w_ref, map_ref,
    states_ref, adjoint_ref, grad_ref,
    fwd_l, adj_l, gath, core_send, core_recv, z_send, z_recv, gath2, q_send, q_recv,
    g_send, g_recv, s_all,
    a_s, a_r, b_s, b_r, c_s, c_r, d_s, d_r, e_s, e_r, f_s, f_r, g_s, g_r, h_s, h_r, i_s, i_r,
):
    r, c = lax.axis_index("row"), lax.axis_index("col")
    n_z = n_row // 2
    plane = 2 * n_col
    z, core = r // 2, r % 2
    other = 1 - core
    nodes, width = state_ref.shape
    slots, block = val_ref.shape[2], val_ref.shape[3]
    place = c * 2 + core

    def z_peer(d):
        return (2 * ((z + d) % n_z) + core, c)

    def plane_peer(e):
        p = (place + e) % plane
        return p, (2 * z + p % 2, p // 2)

    def send(src, dst, s_sem, r_sem, device):
        copy = pltpu.make_async_remote_copy(
            src_ref=src, dst_ref=dst, send_sem=s_sem, recv_sem=r_sem,
            device_id=device, device_id_type=MESH,
        )
        copy.start()
        return copy

    started = []

    barrier = pltpu.get_barrier_semaphore()
    for d in range(1, n_z):
        pl.semaphore_signal(barrier, inc=1, device_id=z_peer(d), device_id_type=MESH)
    for e in range(1, plane):
        pl.semaphore_signal(barrier, inc=1, device_id=plane_peer(e)[1], device_id_type=MESH)

    wide = jnp.broadcast_to(deg_ref[...].astype(F32), (nodes, nodes))
    inv = lax.rsqrt(wide.T)
    inv = jnp.concatenate([inv] * (width // nodes), axis=1)
    gath[c] = (inv * state_ref[...]).astype(BF16)

    pl.semaphore_wait(barrier, n_z - 1 + plane - 1)

    a_copies = []
    for d in range(1, n_col):
        a_copies.append(
            send(gath.at[c], gath.at[c], a_s.at[d - 1], a_r.at[d - 1], (r, (c + d) % n_col))
        )

    for t in range(slots):
        tile = val_ref[0, 0, t].astype(F32)
        turned = tile.T
        at = pl.ds(t * block, block)
        live = live_ref[0, 0, t] == 1
        for k in range(2):
            for d in range(n_z):
                goal = 2 * ((z + d) % n_z) + (other if k == 0 else core)
                keep = jnp.where(live & (cols_ref[0, 0, t] == goal), 1.0, 0.0).astype(F32)
                fwd_l[k, d, :, at] = (turned * keep).astype(BF16)
        for d in range(n_col):
            keep = jnp.where(live & (rows_ref[0, 0, t] == (c + d) % n_col), 1.0, 0.0).astype(F32)
            adj_l[d, :, at] = (tile * keep).astype(BF16)
    feat = feat_ref[...]
    driving = jnp.dot(feat.astype(BF16), map_ref[...].astype(BF16), preferred_element_type=F32)

    for copy in a_copies:
        copy.wait_recv()
    started += a_copies

    picked = jnp.concatenate([gath[rows_ref[0, 0, t]] for t in range(slots)], axis=0)
    order = list(range(1, n_z)) + [0]
    b_copies = {}
    for d in order:
        core_send[d] = jnp.dot(fwd_l[0, d], picked, preferred_element_type=F32).astype(BF16)
        b_copies[d] = send(
            core_send.at[d], core_recv.at[d], b_s.at[d], b_r.at[d], (2 * z + other, c)
        )
    c_copies = []
    for d in order:
        mine = jnp.dot(fwd_l[1, d], picked, preferred_element_type=F32)
        b_copies[d].wait_recv()
        total = mine + core_recv[d].astype(F32)
        if d:
            z_send[d - 1] = total.astype(BF16)
            c_copies.append(
                send(z_send.at[d - 1], z_recv.at[d - 1], c_s.at[d - 1], c_r.at[d - 1], z_peer(d))
            )
    for d in range(1, n_z):
        c_copies[d - 1].wait_recv()
        total = total + z_recv[d - 1].astype(F32)
    started += list(b_copies.values()) + c_copies

    summed = inv * total
    states = jnp.tanh(
        jnp.dot(summed.astype(BF16), w_ref[...].astype(BF16), preferred_element_type=F32) + driving
    )
    slopes = 1.0 - states * states
    cot = cot_ref[...]
    gath2[r] = (inv * (slopes * cot)).astype(BF16)

    d_copies = [
        send(gath2.at[r], gath2.at[r], d_s.at[d - 1], d_r.at[d - 1], z_peer(d))
        for d in range(1, n_z)
    ]
    e_copies = [send(gath2.at[r], gath2.at[r], e_s.at[0], e_r.at[0], (2 * z + other, c))]
    states_ref[...] = states
    both_t = jnp.concatenate([summed.T, feat.T], axis=0).astype(BF16)
    for d in range(1, n_z):
        d_copies[d - 1].wait_recv()
        slot = 2 * ((z + n_z - d) % n_z) + core
        e_copies.append(
            send(gath2.at[slot], gath2.at[slot], e_s.at[d], e_r.at[d], (2 * z + other, c))
        )
    for copy in e_copies:
        copy.wait_recv()
    started += d_copies + e_copies

    picked = jnp.concatenate([gath2[cols_ref[0, 0, t]] for t in range(slots)], axis=0)
    f_copies = []
    for d in range(1, n_col):
        q_send[d - 1] = jnp.dot(adj_l[d], picked, preferred_element_type=F32).astype(BF16)
        f_copies.append(
            send(q_send.at[d - 1], q_recv.at[d - 1], f_s.at[d - 1], f_r.at[d - 1], (r, (c + d) % n_col))
        )
    total = jnp.dot(adj_l[0], picked, preferred_element_type=F32)
    for d in range(1, n_col):
        f_copies[d - 1].wait_recv()
        total = total + q_recv[d - 1].astype(F32)
    started += f_copies
    pulled = inv * total
    adjoint = cot + lax.dot_general(
        pulled.astype(BF16), w_ref[...].astype(BF16), (((1,), (1,)), ((), ())),
        preferred_element_type=F32,
    )
    masked = (slopes * adjoint).astype(BF16)

    grad = jnp.dot(both_t, masked, preferred_element_type=F32)
    g_send[...] = grad.reshape(g_send.shape).astype(BF16)
    g_copies = []
    for e in range(1, plane):
        p, device = plane_peer(e)
        g_copies.append(
            send(g_send.at[p], g_recv.at[e - 1], g_s.at[e - 1], g_r.at[e - 1], device)
        )
    adjoint_ref[...] = adjoint
    total = g_send[place].astype(F32)
    for e in range(1, plane):
        g_copies[e - 1].wait_recv()
        total = total + g_recv[e - 1].astype(F32)
    s_all[z] = total.astype(BF16)
    h_copies = [
        send(s_all.at[z], s_all.at[z], h_s.at[d - 1], h_r.at[d - 1], z_peer(d))
        for d in range(1, n_z)
    ]
    for copy in h_copies:
        copy.wait_recv()
    total = s_all[0].astype(F32)
    for d in range(1, n_z):
        total = total + s_all[d].astype(F32)
    grad_ref[place] = (total * factor).astype(BF16)
    i_copies = [
        send(grad_ref.at[place], grad_ref.at[place], i_s.at[e - 1], i_r.at[e - 1], plane_peer(e)[1])
        for e in range(1, plane)
    ]
    for copy in i_copies:
        copy.wait_recv()
    started += g_copies + h_copies + i_copies
    for copy in started:
        copy.wait_send()


def fits(n_row, n_col, nodes, width, inputs, slots, block):
    plan = 4 * slots * block * block * (n_row + n_col)
    plan += 8 * nodes * width * (n_row + n_col)
    plane = 2 * n_col
    return (
        plan <= VMEM_PLAN
        and nodes == block
        and width % nodes == 0
        and n_row % 2 == 0
        and (width + inputs) % (16 * plane) == 0
    )


def kernel_path(
    starting_state, features, cotangent, degrees, tile_values,
    tile_rows, tile_cols, tile_live, weight, input_map,
):
    n_row, n_col = lax.axis_size("row"), lax.axis_size("col")
    n_z, plane = n_row // 2, 2 * n_col
    nodes, width = starting_state.shape
    inputs = features.shape[1]
    slots, block = tile_values.shape[2], tile_values.shape[3]
    factor = 1.0 / math.sqrt(nodes * n_row * n_col)
    rows_each = (width + inputs) // plane
    vmem = pl.BlockSpec(memory_space=pltpu.VMEM)
    smem = pl.BlockSpec(memory_space=pltpu.SMEM)
    piece = (nodes, width)
    sems = []
    for count in (n_col - 1, n_z, n_z - 1, n_z - 1, n_z, n_col - 1, plane - 1, n_z - 1, plane - 1):
        sems += [pltpu.SemaphoreType.DMA((count,)), pltpu.SemaphoreType.DMA((count,))]
    states, adjoint, grads = pl.pallas_call(
        functools.partial(kernel, n_row, n_col, factor),
        out_shape=(
            jax.ShapeDtypeStruct(piece, F32),
            jax.ShapeDtypeStruct(piece, F32),
            jax.ShapeDtypeStruct((plane, rows_each, width), BF16),
        ),
        in_specs=[vmem] * 5 + [smem] * 3 + [vmem] * 2,
        out_specs=(vmem, vmem, vmem),
        scratch_shapes=[
            pltpu.VMEM((2, n_z, block, slots * block), BF16),
            pltpu.VMEM((n_col, block, slots * block), BF16),
            pltpu.VMEM((n_col,) + piece, BF16),
            pltpu.VMEM((n_z,) + piece, BF16),
            pltpu.VMEM((n_z,) + piece, BF16),
            pltpu.VMEM((n_z - 1,) + piece, BF16),
            pltpu.VMEM((n_z - 1,) + piece, BF16),
            pltpu.VMEM((n_row,) + piece, BF16),
            pltpu.VMEM((n_col - 1,) + piece, BF16),
            pltpu.VMEM((n_col - 1,) + piece, BF16),
            pltpu.VMEM((plane, rows_each, width), BF16),
            pltpu.VMEM((plane - 1, rows_each, width), BF16),
            pltpu.VMEM((n_z, rows_each, width), BF16),
        ] + sems,
        compiler_params=pltpu.CompilerParams(collective_id=0, has_side_effects=True),
        name="graph_window",
    )(
        starting_state, features, cotangent, degrees.reshape(1, -1), tile_values,
        tile_rows, tile_cols, tile_live, weight, input_map,
    )
    grads = grads.reshape(width + inputs, width).astype(F32)
    return states, adjoint, grads[:width], grads[width:]


def on_device(*args):
    nodes, width = args[0].shape
    sizes = (nodes, width, args[1].shape[1], args[4].shape[2], args[4].shape[3])
    if fits(lax.axis_size("row"), lax.axis_size("col"), *sizes):
        return kernel_path(*args)
    return collective_path(*args)


def solution(mesh):
    nodes_split = P(("row", "col"), None)
    tiles_split = P("row", "col", None)
    return jax.shard_map(
        on_device,
        mesh=mesh,
        in_specs=(
            nodes_split, nodes_split, nodes_split, P(("row", "col")),
            P("row", "col", None, None, None), tiles_split, tiles_split, tiles_split, P(), P(),
        ),
        out_specs=(nodes_split, nodes_split, P(), P()),
        check_vma=False,
    )
```

```python
import functools
import math

import jax
import jax.numpy as jnp
from jax import lax
from jax.experimental import pallas as pl
from jax.experimental.pallas import tpu as pltpu
from jax.sharding import PartitionSpec as P

PRECISION_HIGH = lax.Precision.HIGHEST
MESH = pl.DeviceIdType.MESH
VMEM_PLAN = 12 * 2**20
KERNEL_LIMIT = 24 * 2**20
FINISH_LIMIT = 8 * 2**20
F32 = jnp.float32
BF16 = jnp.bfloat16


def spread(values, picked_at, label_at, live_here, gathered, out_count, equation):
    blocks = gathered.reshape(-1, values.shape[1], gathered.shape[1])
    picked = jnp.take(blocks, picked_at, axis=0)
    products = jnp.einsum(equation, values, picked, preferred_element_type=F32)
    labels = jnp.where(live_here == 1, label_at, out_count)
    return jax.ops.segment_sum(products, labels, num_segments=out_count)


def collective_path(
    starting_state, features, cotangent, degrees, tile_values,
    tile_rows, tile_cols, tile_live, weight, input_map,
):
    values, rows_here = tile_values[0, 0], tile_rows[0, 0]
    cols_here, live_here = tile_cols[0, 0], tile_live[0, 0]
    nodes, width = starting_state.shape
    block = values.shape[1]
    n_row, n_col = lax.axis_size("row"), lax.axis_size("col")
    inverse_root = lax.rsqrt(degrees.astype(F32))[:, None]
    driving = jnp.dot(features, input_map, precision=PRECISION_HIGH)
    scaled = (inverse_root * starting_state).astype(BF16)
    gathered = lax.all_gather(scaled, "col", axis=0, tiled=True)
    partial = spread(
        values, rows_here, cols_here, live_here, gathered, n_row * nodes // block, "tab,taf->tbf"
    )
    partial = partial.reshape(n_row * nodes, width).astype(BF16)
    own = lax.psum_scatter(partial, "row", scatter_dimension=0, tiled=True).astype(F32)
    summed = inverse_root * own
    states = jnp.tanh(jnp.dot(summed, weight, precision=PRECISION_HIGH) + driving)
    slopes = 1.0 - states * states
    scaled = (inverse_root * (slopes * cotangent)).astype(BF16)
    gathered = lax.all_gather(scaled, "row", axis=0, tiled=True)
    partial = spread(
        values, cols_here, rows_here, live_here, gathered, n_col * nodes // block, "tab,tbf->taf"
    )
    partial = partial.reshape(n_col * nodes, width).astype(BF16)
    own = lax.psum_scatter(partial, "col", scatter_dimension=0, tiled=True).astype(F32)
    pulled = inverse_root * own
    adjoint = cotangent + jnp.dot(pulled, weight.T, precision=PRECISION_HIGH)
    masked = slopes * adjoint
    factor = 1.0 / math.sqrt(nodes * n_row * n_col)
    weight_part = jnp.dot(summed.T, masked, precision=PRECISION_HIGH)
    input_part = jnp.dot(features.T, masked, precision=PRECISION_HIGH)
    weight_grad, input_grad = lax.psum((weight_part, input_part), ("row", "col"))
    return states, adjoint, weight_grad * factor, input_grad * factor


def kernel(
    n_row, n_col, factor,
    state_in, feat_in, cot_in, deg_in, val_in, rows_in, cols_in, live_in, w_in, map_in,
    states_ref, adjoint_ref, grad_ref,
    state_ref, feat_ref, cot_ref, deg_ref, val_ref, rows_ref, cols_ref, live_ref, w_ref, map_ref, in_sem,
    fwd_l, adj_l, gath, core_send, core_recv, z_send, z_recv, gath2, q_send, q_recv,
    g_send, g_recv, s_all,
    a_s, a_r, b_s, b_r, c_s, c_r, d_s, d_r, e_s, e_r, f_s, f_r, g_s, g_r, h_s, h_r, i_s, i_r,
):
    r, c = lax.axis_index("row"), lax.axis_index("col")
    n_z = n_row // 2
    plane = 2 * n_col
    z, core = r // 2, r % 2
    other = 1 - core
    nodes, width = state_ref.shape
    slots, block = val_ref.shape[2], val_ref.shape[3]
    place = c * 2 + core

    def z_peer(d):
        return (2 * ((z + d) % n_z) + core, c)

    def plane_peer(e):
        p = (place + e) % plane
        return p, (2 * z + p % 2, p // 2)

    def send(src, dst, s_sem, r_sem, device):
        copy = pltpu.make_async_remote_copy(
            src_ref=src, dst_ref=dst, send_sem=s_sem, recv_sem=r_sem,
            device_id=device, device_id_type=MESH,
        )
        copy.start()
        return copy

    started = []

    barrier = pltpu.get_barrier_semaphore()
    for d in range(1, n_z):
        pl.semaphore_signal(barrier, inc=1, device_id=z_peer(d), device_id_type=MESH)
    for e in range(1, plane):
        pl.semaphore_signal(barrier, inc=1, device_id=plane_peer(e)[1], device_id_type=MESH)

    pairs = (
        (deg_in, deg_ref), (state_in, state_ref), (rows_in, rows_ref), (cols_in, cols_ref),
        (live_in, live_ref), (val_in, val_ref), (feat_in, feat_ref), (map_in, map_ref),
        (w_in, w_ref), (cot_in, cot_ref),
    )
    loads = [
        pltpu.make_async_copy(src, dst, in_sem.at[i]) for i, (src, dst) in enumerate(pairs)
    ]
    for load in loads:
        load.start()
    for load in loads[:2]:
        load.wait()

    wide = jnp.broadcast_to(deg_ref[...].astype(F32), (nodes, nodes))
    inv = lax.rsqrt(wide.T)
    inv = jnp.concatenate([inv] * (width // nodes), axis=1)
    gath[c] = (inv * state_ref[...]).astype(BF16)

    pl.semaphore_wait(barrier, n_z - 1 + plane - 1)

    a_copies = []
    for d in range(1, n_col):
        a_copies.append(
            send(gath.at[c], gath.at[c], a_s.at[d - 1], a_r.at[d - 1], (r, (c + d) % n_col))
        )

    for load in loads[2:]:
        load.wait()

    for t in range(slots):
        tile = val_ref[0, 0, t].astype(F32)
        turned = tile.T
        at = pl.ds(t * block, block)
        live = live_ref[0, 0, t] == 1
        for k in range(2):
            for d in range(n_z):
                goal = 2 * ((z + d) % n_z) + (other if k == 0 else core)
                keep = jnp.where(live & (cols_ref[0, 0, t] == goal), 1.0, 0.0).astype(F32)
                fwd_l[k, d, :, at] = (turned * keep).astype(BF16)
        for d in range(n_col):
            keep = jnp.where(live & (rows_ref[0, 0, t] == (c + d) % n_col), 1.0, 0.0).astype(F32)
            adj_l[d, :, at] = (tile * keep).astype(BF16)
    feat = feat_ref[...]
    driving = jnp.dot(feat.astype(BF16), map_ref[...].astype(BF16), preferred_element_type=F32)

    for copy in a_copies:
        copy.wait_recv()
    started += a_copies

    picked = jnp.concatenate([gath[rows_ref[0, 0, t]] for t in range(slots)], axis=0)
    order = list(range(1, n_z)) + [0]
    b_copies = {}
    for d in order:
        core_send[d] = jnp.dot(fwd_l[0, d], picked, preferred_element_type=F32).astype(BF16)
        b_copies[d] = send(
            core_send.at[d], core_recv.at[d], b_s.at[d], b_r.at[d], (2 * z + other, c)
        )
    c_copies = []
    for d in order:
        mine = jnp.dot(fwd_l[1, d], picked, preferred_element_type=F32)
        b_copies[d].wait_recv()
        total = mine + core_recv[d].astype(F32)
        if d:
            z_send[d - 1] = total.astype(BF16)
            c_copies.append(
                send(z_send.at[d - 1], z_recv.at[d - 1], c_s.at[d - 1], c_r.at[d - 1], z_peer(d))
            )
    for d in range(1, n_z):
        c_copies[d - 1].wait_recv()
        total = total + z_recv[d - 1].astype(F32)
    started += list(b_copies.values()) + c_copies

    summed = inv * total
    states = jnp.tanh(
        jnp.dot(summed.astype(BF16), w_ref[...].astype(BF16), preferred_element_type=F32) + driving
    )
    slopes = 1.0 - states * states
    cot = cot_ref[...]
    gath2[r] = (inv * (slopes * cot)).astype(BF16)

    d_copies = [
        send(gath2.at[r], gath2.at[r], d_s.at[d - 1], d_r.at[d - 1], z_peer(d))
        for d in range(1, n_z)
    ]
    e_copies = [send(gath2.at[r], gath2.at[r], e_s.at[0], e_r.at[0], (2 * z + other, c))]
    states_ref[...] = states
    both_t = jnp.concatenate([summed.T, feat.T], axis=0).astype(BF16)
    for d in range(1, n_z):
        d_copies[d - 1].wait_recv()
        slot = 2 * ((z + n_z - d) % n_z) + core
        e_copies.append(
            send(gath2.at[slot], gath2.at[slot], e_s.at[d], e_r.at[d], (2 * z + other, c))
        )
    for copy in e_copies:
        copy.wait_recv()
    started += d_copies + e_copies

    picked = jnp.concatenate([gath2[cols_ref[0, 0, t]] for t in range(slots)], axis=0)
    f_copies = []
    for d in range(1, n_col):
        q_send[d - 1] = jnp.dot(adj_l[d], picked, preferred_element_type=F32).astype(BF16)
        f_copies.append(
            send(q_send.at[d - 1], q_recv.at[d - 1], f_s.at[d - 1], f_r.at[d - 1], (r, (c + d) % n_col))
        )
    total = jnp.dot(adj_l[0], picked, preferred_element_type=F32)
    for d in range(1, n_col):
        f_copies[d - 1].wait_recv()
        total = total + q_recv[d - 1].astype(F32)
    started += f_copies
    pulled = inv * total
    adjoint = cot + lax.dot_general(
        pulled.astype(BF16), w_ref[...].astype(BF16), (((1,), (1,)), ((), ())),
        preferred_element_type=F32,
    )
    masked = (slopes * adjoint).astype(BF16)

    grad = jnp.dot(both_t, masked, preferred_element_type=F32)
    g_send[...] = grad.reshape(g_send.shape).astype(BF16)
    g_copies = []
    for e in range(1, plane):
        p, device = plane_peer(e)
        g_copies.append(
            send(g_send.at[p], g_recv.at[e - 1], g_s.at[e - 1], g_r.at[e - 1], device)
        )
    adjoint_ref[...] = adjoint
    total = g_send[place].astype(F32)
    for e in range(1, plane):
        g_copies[e - 1].wait_recv()
        total = total + g_recv[e - 1].astype(F32)
    s_all[z] = total.astype(BF16)
    h_copies = [
        send(s_all.at[z], s_all.at[z], h_s.at[d - 1], h_r.at[d - 1], z_peer(d))
        for d in range(1, n_z)
    ]
    for copy in h_copies:
        copy.wait_recv()
    total = s_all[0].astype(F32)
    for d in range(1, n_z):
        total = total + s_all[d].astype(F32)
    grad_ref[place] = (total * factor).astype(BF16)
    i_copies = [
        send(grad_ref.at[place], grad_ref.at[place], i_s.at[e - 1], i_r.at[e - 1], plane_peer(e)[1])
        for e in range(1, plane)
    ]
    for copy in i_copies:
        copy.wait_recv()
    started += g_copies + h_copies + i_copies
    for copy in started:
        copy.wait_send()


def finish(states_in, adjoint_in, grads_in, states_out, adjoint_out, weight_out, input_out):
    states_out[...] = states_in[...]
    adjoint_out[...] = adjoint_in[...]
    grads = grads_in[...].astype(F32).reshape(-1, grads_in.shape[2])
    weight_out[...] = grads[: weight_out.shape[0]]
    input_out[...] = grads[weight_out.shape[0] :]


def fits(n_row, n_col, nodes, width, inputs, slots, block):
    plan = 4 * slots * block * block * (n_row + n_col)
    plan += 8 * nodes * width * (n_row + n_col)
    plane = 2 * n_col
    return (
        plan <= VMEM_PLAN
        and nodes == block
        and width % nodes == 0
        and n_row % 2 == 0
        and (width + inputs) % (16 * plane) == 0
    )


def kernel_path(
    starting_state, features, cotangent, degrees, tile_values,
    tile_rows, tile_cols, tile_live, weight, input_map,
):
    n_row, n_col = lax.axis_size("row"), lax.axis_size("col")
    n_z, plane = n_row // 2, 2 * n_col
    nodes, width = starting_state.shape
    inputs = features.shape[1]
    slots, block = tile_values.shape[2], tile_values.shape[3]
    factor = 1.0 / math.sqrt(nodes * n_row * n_col)
    rows_each = (width + inputs) // plane
    vmem = pl.BlockSpec(memory_space=pltpu.VMEM)
    hbm = pl.BlockSpec(memory_space=pltpu.HBM)
    operands = (
        starting_state, features, cotangent, degrees.reshape(1, -1), tile_values,
        tile_rows, tile_cols, tile_live, weight, input_map,
    )
    held = [
        (pltpu.SMEM if 5 <= i < 8 else pltpu.VMEM)(x.shape, x.dtype)
        for i, x in enumerate(operands)
    ]
    piece = (nodes, width)
    sems = []
    for count in (n_col - 1, n_z, n_z - 1, n_z - 1, n_z, n_col - 1, plane - 1, n_z - 1, plane - 1):
        sems += [pltpu.SemaphoreType.DMA((count,)), pltpu.SemaphoreType.DMA((count,))]
    states, adjoint, grads = pl.pallas_call(
        functools.partial(kernel, n_row, n_col, factor),
        out_shape=(
            jax.ShapeDtypeStruct(piece, F32),
            jax.ShapeDtypeStruct(piece, F32),
            jax.ShapeDtypeStruct((plane, rows_each, width), BF16),
        ),
        in_specs=[hbm] * len(operands),
        out_specs=(vmem, vmem, vmem),
        scratch_shapes=held + [
            pltpu.SemaphoreType.DMA((len(operands),)),
            pltpu.VMEM((2, n_z, block, slots * block), BF16),
            pltpu.VMEM((n_col, block, slots * block), BF16),
            pltpu.VMEM((n_col,) + piece, BF16),
            pltpu.VMEM((n_z,) + piece, BF16),
            pltpu.VMEM((n_z,) + piece, BF16),
            pltpu.VMEM((n_z - 1,) + piece, BF16),
            pltpu.VMEM((n_z - 1,) + piece, BF16),
            pltpu.VMEM((n_row,) + piece, BF16),
            pltpu.VMEM((n_col - 1,) + piece, BF16),
            pltpu.VMEM((n_col - 1,) + piece, BF16),
            pltpu.VMEM((plane, rows_each, width), BF16),
            pltpu.VMEM((plane - 1, rows_each, width), BF16),
            pltpu.VMEM((n_z, rows_each, width), BF16),
        ] + sems,
        compiler_params=pltpu.CompilerParams(
            collective_id=0, has_side_effects=True, vmem_limit_bytes=KERNEL_LIMIT
        ),
        name="graph_window",
    )(*[pltpu.with_memory_space_constraint(x, pltpu.HBM) for x in operands])
    return pl.pallas_call(
        finish,
        out_shape=(
            jax.ShapeDtypeStruct(piece, F32),
            jax.ShapeDtypeStruct(piece, F32),
            jax.ShapeDtypeStruct((width, width), F32),
            jax.ShapeDtypeStruct((inputs, width), F32),
        ),
        in_specs=[vmem] * 3,
        out_specs=(vmem,) * 4,
        compiler_params=pltpu.CompilerParams(vmem_limit_bytes=FINISH_LIMIT),
        name="finish",
    )(states, adjoint, grads)


def on_device(*args):
    nodes, width = args[0].shape
    sizes = (nodes, width, args[1].shape[1], args[4].shape[2], args[4].shape[3])
    if fits(lax.axis_size("row"), lax.axis_size("col"), *sizes):
        return kernel_path(*args)
    return collective_path(*args)


def solution(mesh):
    nodes_split = P(("row", "col"), None)
    tiles_split = P("row", "col", None)
    return jax.shard_map(
        on_device,
        mesh=mesh,
        in_specs=(
            nodes_split, nodes_split, nodes_split, P(("row", "col")),
            P("row", "col", None, None, None), tiles_split, tiles_split, tiles_split, P(), P(),
        ),
        out_specs=(nodes_split, nodes_split, P(), P()),
        check_vma=False,
    )
```

```python
import functools
import math

import jax
import jax.numpy as jnp
from jax import lax
from jax.experimental import pallas as pl
from jax.experimental.pallas import tpu as pltpu
from jax.sharding import PartitionSpec as P

PRECISION_HIGH = lax.Precision.HIGHEST
MESH = pl.DeviceIdType.MESH
VMEM_PLAN = 12 * 2**20
KERNEL_LIMIT = 24 * 2**20
FINISH_LIMIT = 8 * 2**20
F32 = jnp.float32
BF16 = jnp.bfloat16
LANES, SUBLANES = 128, 8


def spread(values, picked_at, label_at, live_here, gathered, out_count, equation):
    blocks = gathered.reshape(-1, values.shape[1], gathered.shape[1])
    picked = jnp.take(blocks, picked_at, axis=0)
    products = jnp.einsum(equation, values, picked, preferred_element_type=F32)
    labels = jnp.where(live_here == 1, label_at, out_count)
    return jax.ops.segment_sum(products, labels, num_segments=out_count)


def collective_path(
    starting_state, features, cotangent, degrees, tile_values,
    tile_rows, tile_cols, tile_live, weight, input_map,
):
    values, rows_here = tile_values[0, 0], tile_rows[0, 0]
    cols_here, live_here = tile_cols[0, 0], tile_live[0, 0]
    nodes, width = starting_state.shape
    block = values.shape[1]
    n_row, n_col = lax.axis_size("row"), lax.axis_size("col")
    inverse_root = lax.rsqrt(degrees.astype(F32))[:, None]
    driving = jnp.dot(features, input_map, precision=PRECISION_HIGH)
    scaled = (inverse_root * starting_state).astype(BF16)
    gathered = lax.all_gather(scaled, "col", axis=0, tiled=True)
    partial = spread(
        values, rows_here, cols_here, live_here, gathered, n_row * nodes // block, "tab,taf->tbf"
    )
    partial = partial.reshape(n_row * nodes, width).astype(BF16)
    own = lax.psum_scatter(partial, "row", scatter_dimension=0, tiled=True).astype(F32)
    summed = inverse_root * own
    states = jnp.tanh(jnp.dot(summed, weight, precision=PRECISION_HIGH) + driving)
    slopes = 1.0 - states * states
    scaled = (inverse_root * (slopes * cotangent)).astype(BF16)
    gathered = lax.all_gather(scaled, "row", axis=0, tiled=True)
    partial = spread(
        values, cols_here, rows_here, live_here, gathered, n_col * nodes // block, "tab,tbf->taf"
    )
    partial = partial.reshape(n_col * nodes, width).astype(BF16)
    own = lax.psum_scatter(partial, "col", scatter_dimension=0, tiled=True).astype(F32)
    pulled = inverse_root * own
    adjoint = cotangent + jnp.dot(pulled, weight.T, precision=PRECISION_HIGH)
    masked = slopes * adjoint
    factor = 1.0 / math.sqrt(nodes * n_row * n_col)
    weight_part = jnp.dot(summed.T, masked, precision=PRECISION_HIGH)
    input_part = jnp.dot(features.T, masked, precision=PRECISION_HIGH)
    weight_grad, input_grad = lax.psum((weight_part, input_part), ("row", "col"))
    return states, adjoint, weight_grad * factor, input_grad * factor


def kernel(
    n_row, n_col, factor,
    state_in, feat_in, cot_in, deg_in, val_in, rows_in, cols_in, live_in, w_in, map_in,
    states_ref, adjoint_ref, grad_ref,
    state_ref, feat_ref, cot_ref, deg_ref, val_ref, rows_ref, cols_ref, live_ref, w_ref, map_ref, in_sem,
    fwd_l, adj_l, gath, core_send, core_recv, z_send, z_recv, gath2, q_send, q_recv,
    g_send, g_recv,
    a_s, a_r, b_s, b_r, c_s, c_r, d_s, d_r, e_s, e_r, f_s, f_r, g_s, g_r, h_s, h_r,
):
    r, c = lax.axis_index("row"), lax.axis_index("col")
    n_z = n_row // 2
    z, core = r // 2, r % 2
    other = 1 - core
    nodes, width = state_ref.shape
    slots, block = val_ref.shape[2], val_ref.shape[3]
    n_all = n_row * n_col
    me = r * n_col + c

    def z_peer(d):
        return (2 * ((z + d) % n_z) + core, c)

    def send(src, dst, s_sem, r_sem, device):
        copy = pltpu.make_async_remote_copy(
            src_ref=src, dst_ref=dst, send_sem=s_sem, recv_sem=r_sem,
            device_id=device, device_id_type=MESH,
        )
        copy.start()
        return copy

    started = []

    barrier = pltpu.get_barrier_semaphore()
    for k in range(1, n_all):
        goal = (me + k) % n_all
        pl.semaphore_signal(
            barrier, inc=1, device_id=(goal // n_col, goal % n_col), device_id_type=MESH
        )

    pairs = (
        (deg_in, deg_ref), (state_in, state_ref), (rows_in, rows_ref), (cols_in, cols_ref),
        (live_in, live_ref), (val_in, val_ref), (feat_in, feat_ref), (map_in, map_ref),
        (w_in, w_ref), (cot_in, cot_ref),
    )
    loads = [
        pltpu.make_async_copy(src, dst, in_sem.at[i]) for i, (src, dst) in enumerate(pairs)
    ]
    for load in loads:
        load.start()
    for load in loads[:2]:
        load.wait()

    wide = jnp.broadcast_to(deg_ref[...].astype(F32), (nodes, nodes))
    inv = lax.rsqrt(wide.T)
    inv = jnp.concatenate([inv] * (width // nodes), axis=1)
    gath[c] = (inv * state_ref[...]).astype(BF16)

    pl.semaphore_wait(barrier, n_all - 1)

    a_copies = []
    for d in range(1, n_col):
        a_copies.append(
            send(gath.at[c], gath.at[c], a_s.at[d - 1], a_r.at[d - 1], (r, (c + d) % n_col))
        )

    for load in loads[2:]:
        load.wait()

    for t in range(slots):
        tile = val_ref[0, 0, t].astype(F32)
        turned = tile.T
        at = pl.ds(t * block, block)
        live = live_ref[0, 0, t] == 1
        for k in range(2):
            for d in range(n_z):
                goal = 2 * ((z + d) % n_z) + (other if k == 0 else core)
                keep = jnp.where(live & (cols_ref[0, 0, t] == goal), 1.0, 0.0).astype(F32)
                fwd_l[k, d, :, at] = (turned * keep).astype(BF16)
        for d in range(n_col):
            keep = jnp.where(live & (rows_ref[0, 0, t] == (c + d) % n_col), 1.0, 0.0).astype(F32)
            adj_l[d, :, at] = (tile * keep).astype(BF16)
    feat = feat_ref[...]
    driving = jnp.dot(feat.astype(BF16), map_ref[...].astype(BF16), preferred_element_type=F32)

    for copy in a_copies:
        copy.wait_recv()
    started += a_copies

    picked = jnp.concatenate([gath[rows_ref[0, 0, t]] for t in range(slots)], axis=0)
    order = sorted(range(1, n_z), key=lambda d: -min(d, n_z - d)) + [0]
    b_copies = {}
    for d in order:
        core_send[d] = jnp.dot(fwd_l[0, d], picked, preferred_element_type=F32).astype(BF16)
        b_copies[d] = send(
            core_send.at[d], core_recv.at[d], b_s.at[d], b_r.at[d], (2 * z + other, c)
        )
    c_copies = {}
    for d in order:
        mine = jnp.dot(fwd_l[1, d], picked, preferred_element_type=F32)
        b_copies[d].wait_recv()
        total = mine + core_recv[d].astype(F32)
        if d:
            z_send[d - 1] = total.astype(BF16)
            c_copies[d] = send(
                z_send.at[d - 1], z_recv.at[d - 1], c_s.at[d - 1], c_r.at[d - 1], z_peer(d)
            )
    for d in reversed(order[:-1]):
        c_copies[d].wait_recv()
        total = total + z_recv[d - 1].astype(F32)
    started += list(b_copies.values()) + list(c_copies.values())

    summed = inv * total
    states = jnp.tanh(
        jnp.dot(summed.astype(BF16), w_ref[...].astype(BF16), preferred_element_type=F32) + driving
    )
    slopes = 1.0 - states * states
    cot = cot_ref[...]
    gath2[r] = (inv * (slopes * cot)).astype(BF16)

    d_copies = {
        d: send(gath2.at[r], gath2.at[r], d_s.at[d - 1], d_r.at[d - 1], z_peer(d))
        for d in order[:-1]
    }
    e_copies = [send(gath2.at[r], gath2.at[r], e_s.at[0], e_r.at[0], (2 * z + other, c))]
    states_ref[...] = states
    both_t = jnp.concatenate([summed.T, feat.T], axis=0).astype(BF16)
    for d in reversed(order[:-1]):
        d_copies[d].wait_recv()
        slot = 2 * ((z + n_z - d) % n_z) + core
        e_copies.append(
            send(gath2.at[slot], gath2.at[slot], e_s.at[d], e_r.at[d], (2 * z + other, c))
        )
    for copy in e_copies:
        copy.wait_recv()
    started += list(d_copies.values()) + e_copies

    picked = jnp.concatenate([gath2[cols_ref[0, 0, t]] for t in range(slots)], axis=0)
    f_copies = []
    for d in range(1, n_col):
        q_send[d - 1] = jnp.dot(adj_l[d], picked, preferred_element_type=F32).astype(BF16)
        f_copies.append(
            send(q_send.at[d - 1], q_recv.at[d - 1], f_s.at[d - 1], f_r.at[d - 1], (r, (c + d) % n_col))
        )
    total = jnp.dot(adj_l[0], picked, preferred_element_type=F32)
    for d in range(1, n_col):
        f_copies[d - 1].wait_recv()
        total = total + q_recv[d - 1].astype(F32)
    started += f_copies
    pulled = inv * total
    adjoint = cot + lax.dot_general(
        pulled.astype(BF16), w_ref[...].astype(BF16), (((1,), (1,)), ((), ())),
        preferred_element_type=F32,
    )
    masked = (slopes * adjoint).astype(BF16)

    grad = jnp.dot(both_t, masked, preferred_element_type=F32)
    halves = width // LANES
    groups = n_all // halves
    for h in range(halves):
        part = grad[:, h * LANES : (h + 1) * LANES]
        g_send[h * groups : (h + 1) * groups] = part.reshape((groups,) + g_send.shape[1:]).astype(BF16)

    def scatter(k):
        goal = (me + k) % n_all
        return pltpu.make_async_remote_copy(
            src_ref=g_send.at[goal], dst_ref=g_recv.at[k - 1],
            send_sem=g_s.at[k - 1], recv_sem=g_r.at[k - 1],
            device_id=(goal // n_col, goal % n_col), device_id_type=MESH,
        )

    def gather(k):
        goal = (me + k) % n_all
        return pltpu.make_async_remote_copy(
            src_ref=grad_ref.at[me], dst_ref=grad_ref.at[me],
            send_sem=h_s.at[k - 1], recv_sem=h_r.at[k - 1],
            device_id=(goal // n_col, goal % n_col), device_id_type=MESH,
        )

    for k in range(1, n_all):
        scatter(k).start()
    adjoint_ref[...] = adjoint
    total = g_send[me].astype(F32)
    for k in range(1, n_all):
        scatter(k).wait_recv()
        total = total + g_recv[k - 1].astype(F32)
    grad_ref[me] = (total * factor).astype(BF16)
    for k in range(1, n_all):
        gather(k).start()
    for k in range(1, n_all):
        gather(k).wait_recv()
    for k in range(1, n_all):
        scatter(k).wait_send()
        gather(k).wait_send()
    for copy in started:
        copy.wait_send()


def finish(states_in, adjoint_in, grads_in, states_out, adjoint_out, weight_out, input_out):
    states_out[...] = states_in[...]
    adjoint_out[...] = adjoint_in[...]
    rows, width = weight_out.shape
    halves = width // LANES
    groups = grads_in.shape[0] // halves
    for h in range(halves):
        part = grads_in[h * groups : (h + 1) * groups].astype(F32).reshape(-1, LANES)
        at = pl.ds(h * LANES, LANES)
        weight_out[:, at] = part[:rows]
        input_out[:, at] = part[rows:]


def fits(n_row, n_col, nodes, width, inputs, slots, block):
    plan = 4 * slots * block * block * (n_row + n_col)
    plan += 8 * nodes * width * (n_row + n_col)
    groups = n_row * n_col // max(width // LANES, 1)
    return (
        plan <= VMEM_PLAN
        and nodes == block
        and width % nodes == 0
        and n_row % 2 == 0
        and width % LANES == 0
        and groups * (width // LANES) == n_row * n_col
        and (width + inputs) % (SUBLANES * groups) == 0
    )


def kernel_path(
    starting_state, features, cotangent, degrees, tile_values,
    tile_rows, tile_cols, tile_live, weight, input_map,
):
    n_row, n_col = lax.axis_size("row"), lax.axis_size("col")
    n_z, n_all = n_row // 2, n_row * n_col
    nodes, width = starting_state.shape
    inputs = features.shape[1]
    slots, block = tile_values.shape[2], tile_values.shape[3]
    factor = 1.0 / math.sqrt(nodes * n_row * n_col)
    shard = ((width + inputs) * width // LANES // n_all, LANES)
    vmem = pl.BlockSpec(memory_space=pltpu.VMEM)
    hbm = pl.BlockSpec(memory_space=pltpu.HBM)
    operands = (
        starting_state, features, cotangent, degrees.reshape(1, -1), tile_values,
        tile_rows, tile_cols, tile_live, weight, input_map,
    )
    held = [
        (pltpu.SMEM if 5 <= i < 8 else pltpu.VMEM)(x.shape, x.dtype)
        for i, x in enumerate(operands)
    ]
    piece = (nodes, width)
    sems = []
    for count in (n_col - 1, n_z, n_z - 1, n_z - 1, n_z, n_col - 1, n_all - 1, n_all - 1):
        sems += [pltpu.SemaphoreType.DMA((count,)), pltpu.SemaphoreType.DMA((count,))]
    states, adjoint, grads = pl.pallas_call(
        functools.partial(kernel, n_row, n_col, factor),
        out_shape=(
            jax.ShapeDtypeStruct(piece, F32),
            jax.ShapeDtypeStruct(piece, F32),
            jax.ShapeDtypeStruct((n_all,) + shard, BF16),
        ),
        in_specs=[hbm] * len(operands),
        out_specs=(vmem, vmem, vmem),
        scratch_shapes=held + [
            pltpu.SemaphoreType.DMA((len(operands),)),
            pltpu.VMEM((2, n_z, block, slots * block), BF16),
            pltpu.VMEM((n_col, block, slots * block), BF16),
            pltpu.VMEM((n_col,) + piece, BF16),
            pltpu.VMEM((n_z,) + piece, BF16),
            pltpu.VMEM((n_z,) + piece, BF16),
            pltpu.VMEM((n_z - 1,) + piece, BF16),
            pltpu.VMEM((n_z - 1,) + piece, BF16),
            pltpu.VMEM((n_row,) + piece, BF16),
            pltpu.VMEM((n_col - 1,) + piece, BF16),
            pltpu.VMEM((n_col - 1,) + piece, BF16),
            pltpu.VMEM((n_all,) + shard, BF16),
            pltpu.VMEM((n_all - 1,) + shard, BF16),
        ] + sems,
        compiler_params=pltpu.CompilerParams(
            collective_id=0, has_side_effects=True, vmem_limit_bytes=KERNEL_LIMIT
        ),
        name="graph_window",
    )(*[pltpu.with_memory_space_constraint(x, pltpu.HBM) for x in operands])
    return pl.pallas_call(
        finish,
        out_shape=(
            jax.ShapeDtypeStruct(piece, F32),
            jax.ShapeDtypeStruct(piece, F32),
            jax.ShapeDtypeStruct((width, width), F32),
            jax.ShapeDtypeStruct((inputs, width), F32),
        ),
        in_specs=[vmem] * 3,
        out_specs=(vmem,) * 4,
        compiler_params=pltpu.CompilerParams(vmem_limit_bytes=FINISH_LIMIT),
        name="finish",
    )(states, adjoint, grads)


def on_device(*args):
    nodes, width = args[0].shape
    sizes = (nodes, width, args[1].shape[1], args[4].shape[2], args[4].shape[3])
    if fits(lax.axis_size("row"), lax.axis_size("col"), *sizes):
        return kernel_path(*args)
    return collective_path(*args)


def solution(mesh):
    nodes_split = P(("row", "col"), None)
    tiles_split = P("row", "col", None)
    return jax.shard_map(
        on_device,
        mesh=mesh,
        in_specs=(
            nodes_split, nodes_split, nodes_split, P(("row", "col")),
            P("row", "col", None, None, None), tiles_split, tiles_split, tiles_split, P(), P(),
        ),
        out_specs=(nodes_split, nodes_split, P(), P()),
        check_vma=False,
    )
```

```python
import functools
import math

import jax
import jax.numpy as jnp
from jax import lax
from jax.experimental import pallas as pl
from jax.experimental.pallas import tpu as pltpu
from jax.sharding import PartitionSpec as P

PRECISION_HIGH = lax.Precision.HIGHEST
MESH = pl.DeviceIdType.MESH
VMEM_PLAN = 12 * 2**20
KERNEL_LIMIT = 24 * 2**20
FINISH_LIMIT = 8 * 2**20
F32 = jnp.float32
BF16 = jnp.bfloat16


def spread(values, picked_at, label_at, live_here, gathered, out_count, equation):
    blocks = gathered.reshape(-1, values.shape[1], gathered.shape[1])
    picked = jnp.take(blocks, picked_at, axis=0)
    products = jnp.einsum(equation, values, picked, preferred_element_type=F32)
    labels = jnp.where(live_here == 1, label_at, out_count)
    return jax.ops.segment_sum(products, labels, num_segments=out_count)


def collective_path(
    starting_state, features, cotangent, degrees, tile_values,
    tile_rows, tile_cols, tile_live, weight, input_map,
):
    values, rows_here = tile_values[0, 0], tile_rows[0, 0]
    cols_here, live_here = tile_cols[0, 0], tile_live[0, 0]
    nodes, width = starting_state.shape
    block = values.shape[1]
    n_row, n_col = lax.axis_size("row"), lax.axis_size("col")
    inverse_root = lax.rsqrt(degrees.astype(F32))[:, None]
    driving = jnp.dot(features, input_map, precision=PRECISION_HIGH)
    scaled = (inverse_root * starting_state).astype(BF16)
    gathered = lax.all_gather(scaled, "col", axis=0, tiled=True)
    partial = spread(
        values, rows_here, cols_here, live_here, gathered, n_row * nodes // block, "tab,taf->tbf"
    )
    partial = partial.reshape(n_row * nodes, width).astype(BF16)
    own = lax.psum_scatter(partial, "row", scatter_dimension=0, tiled=True).astype(F32)
    summed = inverse_root * own
    states = jnp.tanh(jnp.dot(summed, weight, precision=PRECISION_HIGH) + driving)
    slopes = 1.0 - states * states
    scaled = (inverse_root * (slopes * cotangent)).astype(BF16)
    gathered = lax.all_gather(scaled, "row", axis=0, tiled=True)
    partial = spread(
        values, cols_here, rows_here, live_here, gathered, n_col * nodes // block, "tab,tbf->taf"
    )
    partial = partial.reshape(n_col * nodes, width).astype(BF16)
    own = lax.psum_scatter(partial, "col", scatter_dimension=0, tiled=True).astype(F32)
    pulled = inverse_root * own
    adjoint = cotangent + jnp.dot(pulled, weight.T, precision=PRECISION_HIGH)
    masked = slopes * adjoint
    factor = 1.0 / math.sqrt(nodes * n_row * n_col)
    weight_part = jnp.dot(summed.T, masked, precision=PRECISION_HIGH)
    input_part = jnp.dot(features.T, masked, precision=PRECISION_HIGH)
    weight_grad, input_grad = lax.psum((weight_part, input_part), ("row", "col"))
    return states, adjoint, weight_grad * factor, input_grad * factor


def kernel(
    n_row, n_col, factor,
    state_in, feat_in, cot_in, deg_in, val_in, rows_in, cols_in, live_in, w_in, map_in,
    states_ref, adjoint_ref, grad_ref,
    state_ref, feat_ref, cot_ref, deg_ref, val_ref, rows_ref, cols_ref, live_ref, w_ref, map_ref, in_sem,
    fwd_l, adj_l, gath, core_send, core_recv, z_send, z_recv, gath2, q_send, q_recv,
    both_t, gx_send, gx_recv, g_send, g_recv, s_all,
    a_s, a_r, b_s, b_r, c_s, c_r, d_s, d_r, e_s, e_r, f_s, f_r, g_s, g_r, h_s, h_r, i_s, i_r, gx_s, gx_r, j_s, j_r,
):
    r, c = lax.axis_index("row"), lax.axis_index("col")
    n_z = n_row // 2
    z, core = r // 2, r % 2
    other = 1 - core
    nodes, width = state_ref.shape
    slots, block = val_ref.shape[2], val_ref.shape[3]

    def z_peer(d):
        return (2 * ((z + d) % n_z) + core, c)

    def send(src, dst, s_sem, r_sem, device):
        copy = pltpu.make_async_remote_copy(
            src_ref=src, dst_ref=dst, send_sem=s_sem, recv_sem=r_sem,
            device_id=device, device_id_type=MESH,
        )
        copy.start()
        return copy

    started = []

    barrier = pltpu.get_barrier_semaphore()
    for d in range(1, n_z):
        pl.semaphore_signal(barrier, inc=1, device_id=z_peer(d), device_id_type=MESH)
    for d in range(1, n_col):
        pl.semaphore_signal(barrier, inc=1, device_id=(r, (c + d) % n_col), device_id_type=MESH)
    pl.semaphore_signal(barrier, inc=1, device_id=(2 * z + other, c), device_id_type=MESH)

    pairs = (
        (deg_in, deg_ref), (state_in, state_ref), (rows_in, rows_ref), (cols_in, cols_ref),
        (live_in, live_ref), (val_in, val_ref), (feat_in, feat_ref), (map_in, map_ref),
        (w_in, w_ref), (cot_in, cot_ref),
    )
    loads = [
        pltpu.make_async_copy(src, dst, in_sem.at[i]) for i, (src, dst) in enumerate(pairs)
    ]
    for load in loads:
        load.start()
    for load in loads[:2]:
        load.wait()

    wide = jnp.broadcast_to(deg_ref[...].astype(F32), (nodes, nodes))
    inv = lax.rsqrt(wide.T)
    inv = jnp.concatenate([inv] * (width // nodes), axis=1)
    gath[c] = (inv * state_ref[...]).astype(BF16)

    pl.semaphore_wait(barrier, n_z - 1 + n_col - 1 + 1)

    a_copies = []
    for d in range(1, n_col):
        a_copies.append(
            send(gath.at[c], gath.at[c], a_s.at[d - 1], a_r.at[d - 1], (r, (c + d) % n_col))
        )

    for load in loads[2:]:
        load.wait()

    for t in range(slots):
        tile = val_ref[0, 0, t].astype(F32)
        turned = tile.T
        at = pl.ds(t * block, block)
        live = live_ref[0, 0, t] == 1
        for k in range(2):
            for d in range(n_z):
                goal = 2 * ((z + d) % n_z) + (other if k == 0 else core)
                keep = jnp.where(live & (cols_ref[0, 0, t] == goal), 1.0, 0.0).astype(F32)
                fwd_l[k, d, :, at] = (turned * keep).astype(BF16)
        for d in range(n_col):
            keep = jnp.where(live & (rows_ref[0, 0, t] == (c + d) % n_col), 1.0, 0.0).astype(F32)
            adj_l[d, :, at] = (tile * keep).astype(BF16)
    feat = feat_ref[...]
    driving = jnp.dot(feat.astype(BF16), map_ref[...].astype(BF16), preferred_element_type=F32)

    for copy in a_copies:
        copy.wait_recv()
    started += a_copies

    picked = jnp.concatenate([gath[rows_ref[0, 0, t]] for t in range(slots)], axis=0)
    order = sorted(range(1, n_z), key=lambda d: -min(d, n_z - d)) + [0]
    b_copies = {}
    for d in order:
        core_send[d] = jnp.dot(fwd_l[0, d], picked, preferred_element_type=F32).astype(BF16)
        b_copies[d] = send(
            core_send.at[d], core_recv.at[d], b_s.at[d], b_r.at[d], (2 * z + other, c)
        )
    c_copies = {}
    for d in order:
        mine = jnp.dot(fwd_l[1, d], picked, preferred_element_type=F32)
        b_copies[d].wait_recv()
        total = mine + core_recv[d].astype(F32)
        if d:
            z_send[d - 1] = total.astype(BF16)
            c_copies[d] = send(
                z_send.at[d - 1], z_recv.at[d - 1], c_s.at[d - 1], c_r.at[d - 1], z_peer(d)
            )
    for d in reversed(order[:-1]):
        c_copies[d].wait_recv()
        total = total + z_recv[d - 1].astype(F32)
    started += list(b_copies.values()) + list(c_copies.values())

    summed = inv * total
    states = jnp.tanh(
        jnp.dot(summed.astype(BF16), w_ref[...].astype(BF16), preferred_element_type=F32) + driving
    )
    slopes = 1.0 - states * states
    cot = cot_ref[...]
    gath2[r] = (inv * (slopes * cot)).astype(BF16)

    d_copies = [
        send(gath2.at[r], gath2.at[r], d_s.at[d - 1], d_r.at[d - 1], z_peer(d))
        for d in range(1, n_z)
    ]
    e_copies = [send(gath2.at[r], gath2.at[r], e_s.at[0], e_r.at[0], (2 * z + other, c))]
    states_ref[...] = states
    both_t[...] = jnp.concatenate([summed.T, feat.T], axis=0).reshape(both_t.shape).astype(BF16)
    for d in range(1, n_z):
        d_copies[d - 1].wait_recv()
        slot = 2 * ((z + n_z - d) % n_z) + core
        e_copies.append(
            send(gath2.at[slot], gath2.at[slot], e_s.at[d], e_r.at[d], (2 * z + other, c))
        )
    for copy in e_copies:
        copy.wait_recv()
    started += d_copies + e_copies

    picked = jnp.concatenate([gath2[cols_ref[0, 0, t]] for t in range(slots)], axis=0)
    f_copies = []
    for d in range(1, n_col):
        q_send[d - 1] = jnp.dot(adj_l[d], picked, preferred_element_type=F32).astype(BF16)
        f_copies.append(
            send(q_send.at[d - 1], q_recv.at[d - 1], f_s.at[d - 1], f_r.at[d - 1], (r, (c + d) % n_col))
        )
    total = jnp.dot(adj_l[0], picked, preferred_element_type=F32)
    for d in range(1, n_col):
        f_copies[d - 1].wait_recv()
        total = total + q_recv[d - 1].astype(F32)
    started += f_copies
    pulled = inv * total
    adjoint = cot + lax.dot_general(
        pulled.astype(BF16), w_ref[...].astype(BF16), (((1,), (1,)), ((), ())),
        preferred_element_type=F32,
    )
    masked = (slopes * adjoint).astype(BF16)

    gx_send[...] = (
        jnp.dot(both_t[other], masked, preferred_element_type=F32).reshape(gx_send.shape).astype(BF16)
    )
    gx_copy = send(gx_send, gx_recv, gx_s.at[0], gx_r.at[0], (2 * z + other, c))
    grad = jnp.dot(both_t[core], masked, preferred_element_type=F32).reshape(g_send.shape)
    adjoint_ref[...] = adjoint
    gx_copy.wait_recv()
    g_send[...] = (grad + gx_recv[...].astype(F32)).astype(BF16)
    g_copies = []
    for d in range(1, n_col):
        goal = (c + d) % n_col
        g_copies.append(
            send(g_send.at[goal], g_recv.at[d - 1], g_s.at[d - 1], g_r.at[d - 1], (r, goal))
        )
    total = g_send[c].astype(F32)
    for d in range(1, n_col):
        g_copies[d - 1].wait_recv()
        total = total + g_recv[d - 1].astype(F32)
    s_all[z] = total.astype(BF16)
    h_copies = [
        send(s_all.at[z], s_all.at[z], h_s.at[d - 1], h_r.at[d - 1], z_peer(d))
        for d in range(1, n_z)
    ]
    for copy in h_copies:
        copy.wait_recv()
    total = s_all[0].astype(F32)
    for d in range(1, n_z):
        total = total + s_all[d].astype(F32)
    mine = core * n_col + c
    grad_ref[mine] = (total * factor).astype(BF16)

    i_copies = [
        send(grad_ref.at[mine], grad_ref.at[mine], i_s.at[d - 1], i_r.at[d - 1], (r, (c + d) % n_col))
        for d in range(1, n_col)
    ]
    j_copies = [
        send(grad_ref.at[mine], grad_ref.at[mine], j_s.at[0], j_r.at[0], (2 * z + other, c))
    ]
    for d in range(1, n_col):
        i_copies[d - 1].wait_recv()
        slot = core * n_col + (c + n_col - d) % n_col
        j_copies.append(
            send(grad_ref.at[slot], grad_ref.at[slot], j_s.at[d], j_r.at[d], (2 * z + other, c))
        )
    for copy in j_copies:
        copy.wait_recv()
    started += [gx_copy] + g_copies + h_copies + i_copies + j_copies
    for copy in started:
        copy.wait_send()


def finish(states_in, adjoint_in, grads_in, states_out, adjoint_out, weight_out, input_out):
    states_out[...] = states_in[...]
    adjoint_out[...] = adjoint_in[...]
    grads = grads_in[...].astype(F32).reshape(-1, grads_in.shape[2])
    weight_out[...] = grads[: weight_out.shape[0]]
    input_out[...] = grads[weight_out.shape[0] :]


def fits(n_row, n_col, nodes, width, inputs, slots, block):
    plan = 4 * slots * block * block * (n_row + n_col)
    plan += 8 * nodes * width * (n_row + n_col)
    plane = 2 * n_col
    return (
        plan <= VMEM_PLAN
        and nodes == block
        and width % nodes == 0
        and n_row % 2 == 0
        and (width + inputs) % (16 * plane) == 0
    )


def kernel_path(
    starting_state, features, cotangent, degrees, tile_values,
    tile_rows, tile_cols, tile_live, weight, input_map,
):
    n_row, n_col = lax.axis_size("row"), lax.axis_size("col")
    n_z, plane = n_row // 2, 2 * n_col
    nodes, width = starting_state.shape
    inputs = features.shape[1]
    slots, block = tile_values.shape[2], tile_values.shape[3]
    factor = 1.0 / math.sqrt(nodes * n_row * n_col)
    rows_each = (width + inputs) // plane
    vmem = pl.BlockSpec(memory_space=pltpu.VMEM)
    hbm = pl.BlockSpec(memory_space=pltpu.HBM)
    operands = (
        starting_state, features, cotangent, degrees.reshape(1, -1), tile_values,
        tile_rows, tile_cols, tile_live, weight, input_map,
    )
    held = [
        (pltpu.SMEM if 5 <= i < 8 else pltpu.VMEM)(x.shape, x.dtype)
        for i, x in enumerate(operands)
    ]
    piece = (nodes, width)
    sems = []
    for count in (n_col - 1, n_z, n_z - 1, n_z - 1, n_z, n_col - 1, n_col - 1, n_z - 1, n_col - 1, 1, n_col):
        sems += [pltpu.SemaphoreType.DMA((count,)), pltpu.SemaphoreType.DMA((count,))]
    states, adjoint, grads = pl.pallas_call(
        functools.partial(kernel, n_row, n_col, factor),
        out_shape=(
            jax.ShapeDtypeStruct(piece, F32),
            jax.ShapeDtypeStruct(piece, F32),
            jax.ShapeDtypeStruct((plane, rows_each, width), BF16),
        ),
        in_specs=[hbm] * len(operands),
        out_specs=(vmem, vmem, vmem),
        scratch_shapes=held + [
            pltpu.SemaphoreType.DMA((len(operands),)),
            pltpu.VMEM((2, n_z, block, slots * block), BF16),
            pltpu.VMEM((n_col, block, slots * block), BF16),
            pltpu.VMEM((n_col,) + piece, BF16),
            pltpu.VMEM((n_z,) + piece, BF16),
            pltpu.VMEM((n_z,) + piece, BF16),
            pltpu.VMEM((n_z - 1,) + piece, BF16),
            pltpu.VMEM((n_z - 1,) + piece, BF16),
            pltpu.VMEM((n_row,) + piece, BF16),
            pltpu.VMEM((n_col - 1,) + piece, BF16),
            pltpu.VMEM((n_col - 1,) + piece, BF16),
            pltpu.VMEM((2, (width + inputs) // 2, nodes), BF16),
            pltpu.VMEM((n_col, rows_each, width), BF16),
            pltpu.VMEM((n_col, rows_each, width), BF16),
            pltpu.VMEM((n_col, rows_each, width), BF16),
            pltpu.VMEM((n_col - 1, rows_each, width), BF16),
            pltpu.VMEM((n_z, rows_each, width), BF16),
        ] + sems,
        compiler_params=pltpu.CompilerParams(
            collective_id=0, has_side_effects=True, vmem_limit_bytes=KERNEL_LIMIT
        ),
        name="graph_window",
    )(*[pltpu.with_memory_space_constraint(x, pltpu.HBM) for x in operands])
    return pl.pallas_call(
        finish,
        out_shape=(
            jax.ShapeDtypeStruct(piece, F32),
            jax.ShapeDtypeStruct(piece, F32),
            jax.ShapeDtypeStruct((width, width), F32),
            jax.ShapeDtypeStruct((inputs, width), F32),
        ),
        in_specs=[vmem] * 3,
        out_specs=(vmem,) * 4,
        compiler_params=pltpu.CompilerParams(vmem_limit_bytes=FINISH_LIMIT),
        name="finish",
    )(states, adjoint, grads)


def on_device(*args):
    nodes, width = args[0].shape
    sizes = (nodes, width, args[1].shape[1], args[4].shape[2], args[4].shape[3])
    if fits(lax.axis_size("row"), lax.axis_size("col"), *sizes):
        return kernel_path(*args)
    return collective_path(*args)


def solution(mesh):
    nodes_split = P(("row", "col"), None)
    tiles_split = P("row", "col", None)
    return jax.shard_map(
        on_device,
        mesh=mesh,
        in_specs=(
            nodes_split, nodes_split, nodes_split, P(("row", "col")),
            P("row", "col", None, None, None), tiles_split, tiles_split, tiles_split, P(), P(),
        ),
        out_specs=(nodes_split, nodes_split, P(), P()),
        check_vma=False,
    )
```
